32 devices in a mesh: ep: 16 (over z, y, x), dp: 2 (over core).
Axes of the slice: x: 2, y: 2, z: 4, core: 2. Of those that a mesh axis runs over, the one named last changes fastest.
Arguments:
- tokens: bfloat16 [4096, 1024], P(('ep', 'dp')), may hold values from -6 to 6
- grad_out: bfloat16 [4096, 1024], P(('ep', 'dp')), may hold values from -3 to 3
- assign: int32 [4096, 2], P(('ep', 'dp')), may hold values from 0 to 15, as said below
- router_weight: bfloat16 [16, 1024], P('ep'), may hold values from -0.1875 to 0.1875
- w_gate: bfloat16 [16, 1024, 2048], P('ep', None, 'dp'), may hold values from -0.1875 to 0.1875
- w_up: bfloat16 [16, 1024, 2048], P('ep', None, 'dp'), may hold values from -0.1875 to 0.1875
- w_down: bfloat16 [16, 2048, 1024], P('ep', 'dp'), may hold values from -0.125 to 0.125
Outputs:
- grad_tokens: bfloat16 [4096, 1024], P(('ep', 'dp'))
- grad_router: float32 [16, 1024], P('ep')
- grad_gate: bfloat16 [16, 1024, 2048], P('ep', None, 'dp')
- grad_up: bfloat16 [16, 1024, 2048], P('ep', None, 'dp')
- grad_down: bfloat16 [16, 2048, 1024], P('ep', 'dp')
The draws below stay inside these ranges and needn't reach their ends.
Inputs may be any that keep to these rules, and one draw needn't show every extreme that they name: `assign`: in each aligned block of 128 rows (the rows of one device) the two experts of a row differ and no expert is named by more than 24 entries; in every block one expert, the same for all blocks, is named by exactly 24 entries.
All inputs are finite; a program needn't handle non-finite values.
Results may differ from the reference program's by a relative error of at most 0.007.
Values may be sent and summed in bfloat16 or wider, within the bound.
A program may use at most 192 MiB of HBM per device.

```python
import jax
import jax.numpy as jnp
from jax import lax

D = 1024
FF = 2048
TOK_DEV = 128
EXPERTS = 16
TOKENS = 4096
CAP = 24


def draw_assign(key, part):
    blocks = TOKENS // TOK_DEV
    rank_key, block_key = jax.random.split(key)
    ordered = jax.random.permutation(rank_key, EXPERTS).astype(jnp.int32)
    favour = jnp.zeros((EXPERTS,), jnp.int32).at[ordered].set(jnp.arange(EXPERTS, dtype=jnp.int32))

    def one_block(bkey):
        noise_key, perm_key, flip_key = jax.random.split(bkey, 3)
        noise = jax.random.randint(noise_key, (EXPERTS,), 0, 4 * EXPERTS, dtype=jnp.int32)
        score = (noise + 4 * (EXPERTS - favour)) * EXPERTS + jnp.arange(EXPERTS, dtype=jnp.int32)
        score = jnp.where(favour == 0, 9 * EXPERTS * EXPERTS, score)
        order = jnp.argsort(-score, stable=True).astype(jnp.int32)
        labels = order[jnp.arange(2 * TOK_DEV, dtype=jnp.int32) // CAP]
        pairs = jnp.stack([labels[:TOK_DEV], labels[TOK_DEV:]], axis=1)
        perm = jax.random.permutation(perm_key, TOK_DEV)
        pairs = pairs[perm]
        flip = jax.random.randint(flip_key, (TOK_DEV, 1), 0, 2, dtype=jnp.int32)
        return jnp.where(flip == 1, pairs[:, ::-1], pairs)
    keys = jax.random.split(block_key, blocks)
    return jax.vmap(one_block)(keys).reshape(TOKENS, 2).astype(jnp.int32)


def steps_of(key, shape, shards, smallest, largest):
    level = 1.0
    for position, parts in shards:
        draws = jax.random.uniform(jax.random.fold_in(jax.random.fold_in(key, 6), position), (parts,), jnp.float32, smallest / len(shards), largest / len(shards))
        level = level * jnp.repeat(jnp.exp(draws), shape[position] // parts).reshape((-1,) + (1,) * (len(shape) - 1 - position))
    return level


def centred(stream_key, shape, spread, reach, pieces=(), held_as=jnp.bfloat16):
    drawn = spread * jax.random.normal(stream_key, shape, jnp.float32)
    if pieces:
        drawn = drawn * steps_of(stream_key, shape, pieces, -0.22, 0.18)
    return jnp.clip(drawn, -reach, reach).astype(held_as)


def setup_inputs(seed: int = 0) -> dict:
    arg_keys = jax.random.split(jax.random.key(seed), 8)
    return {
        "tokens": centred(arg_keys[0], (TOKENS, D), 1.0, 6.0, ((0, 32),)),
        "grad_out": centred(arg_keys[1], (TOKENS, D), 0.5, 3.0, ((0, 32),)),
        "assign": draw_assign(jax.random.fold_in(arg_keys[7], 71), 0),
        "router_weight": centred(arg_keys[3], (EXPERTS, D), D ** -0.5, 0.1875, ((0, 16),)),
        "w_gate": centred(arg_keys[4], (EXPERTS, D, FF), D ** -0.5, 0.1875, ((0, 16), (2, 2))),
        "w_up": centred(arg_keys[5], (EXPERTS, D, FF), D ** -0.5, 0.1875, ((0, 16), (2, 2))),
        "w_down": centred(arg_keys[6], (EXPERTS, FF, D), FF ** -0.5, 0.125, ((0, 16), (1, 2))),
    }


def entry_slots(assign, experts, cap):
    flat = assign.reshape(-1).astype(jnp.int32)
    marks = (flat[:, None] == jnp.arange(experts, dtype=jnp.int32)[None, :]).astype(jnp.int32)
    before = jnp.cumsum(marks, axis=0) - marks
    ranks = jnp.sum(before * marks, axis=1).astype(jnp.int32)
    return (flat * cap + ranks).astype(jnp.int32)


def expert_grads(rows, upstream, gate_vals, wg, wu, wd):
    pre_a = jnp.dot(rows, wg, preferred_element_type=jnp.float32)
    pre_b = jnp.dot(rows, wu, preferred_element_type=jnp.float32)
    sigma = jax.nn.sigmoid(pre_a)
    active = pre_a * sigma
    hidden = (active * pre_b).astype(jnp.bfloat16)
    outer = jnp.dot(hidden, wd, preferred_element_type=jnp.float32)
    up_f = upstream.astype(jnp.float32)
    grad_gates = jnp.sum(up_f * outer, axis=1)
    scaled = (gate_vals.astype(jnp.float32)[:, None] * up_f).astype(jnp.bfloat16)
    grad_hidden = jnp.dot(scaled, wd.T, preferred_element_type=jnp.float32)
    grad_a = (grad_hidden * pre_b * sigma * (1.0 + pre_a * (1.0 - sigma))).astype(jnp.bfloat16)
    grad_b = (grad_hidden * active).astype(jnp.bfloat16)
    grad_rows = jnp.dot(grad_a, wg.T, preferred_element_type=jnp.float32) + jnp.dot(grad_b, wu.T, preferred_element_type=jnp.float32)
    g_gate = jnp.dot(rows.T, grad_a, preferred_element_type=jnp.float32)
    g_up = jnp.dot(rows.T, grad_b, preferred_element_type=jnp.float32)
    g_down = jnp.dot(hidden.T, scaled, preferred_element_type=jnp.float32)
    return grad_rows, grad_gates, g_gate, g_up, g_down


def reference(tokens, grad_out, assign, router_weight, w_gate, w_up, w_down):
    blocks = TOKENS // TOK_DEV
    entries = 2 * TOK_DEV
    choose = (assign[:, :, None] == jnp.arange(EXPERTS, dtype=jnp.int32)[None, None, :]).astype(jnp.float32)
    picked = jnp.sum(tokens.astype(jnp.float32)[:, None, :] * router_weight.astype(jnp.float32)[assign], axis=2)
    sig = jax.nn.sigmoid(picked)
    total = jnp.sum(sig, axis=1, keepdims=True)
    gates = sig / total
    gate_low = gates.reshape(-1).astype(jnp.bfloat16)
    slots = jax.vmap(lambda a: entry_slots(a, EXPERTS, CAP))(assign.reshape(blocks, TOK_DEV, 2))
    table = jnp.full((blocks, EXPERTS * CAP), -1, dtype=jnp.int32)
    block_ids = jnp.arange(blocks, dtype=jnp.int32)[:, None]
    table = table.at[block_ids, slots].set(jnp.arange(blocks * entries, dtype=jnp.int32).reshape(blocks, entries))
    per_expert_ids = table.reshape(blocks, EXPERTS, CAP).transpose(1, 0, 2).reshape(EXPERTS, blocks * CAP)
    zero_low = jnp.zeros((), jnp.bfloat16)

    def one_expert(packed):
        ids, wg, wu, wd = packed
        valid = ids >= 0
        safe = jnp.maximum(ids, 0)
        rows = jnp.where(valid[:, None], tokens[safe // 2], zero_low)
        ups = jnp.where(valid[:, None], grad_out[safe // 2], zero_low)
        gts = jnp.where(valid, gate_low[safe], zero_low)
        grad_rows, grad_gates, g_gate, g_up, g_down = expert_grads(rows, ups, gts, wg, wu, wd)
        return (grad_rows.astype(jnp.bfloat16), grad_gates.astype(jnp.bfloat16), g_gate.astype(jnp.bfloat16), g_up.astype(jnp.bfloat16), g_down.astype(jnp.bfloat16))

    rows_all, gates_all, grad_gate, grad_up, grad_down = lax.map(one_expert, (per_expert_ids, w_gate, w_up, w_down))
    where_to = (slots // CAP) * (blocks * CAP) + block_ids * CAP + slots % CAP
    where_to = where_to.reshape(-1).astype(jnp.int32)
    entry_rows = rows_all.reshape(EXPERTS * blocks * CAP, D)[where_to].astype(jnp.float32).reshape(TOKENS, 2, D)
    entry_gates = gates_all.reshape(-1)[where_to].astype(jnp.float32).reshape(TOKENS, 2)
    mixed = jnp.sum(gates * entry_gates, axis=1, keepdims=True)
    grad_logit = (entry_gates - mixed) / total * sig * (1.0 - sig)
    dense = jnp.sum(grad_logit[:, :, None] * choose, axis=1)
    router_term = jnp.dot(dense, router_weight.astype(jnp.float32), precision=lax.Precision.HIGHEST)
    grad_tokens = (jnp.sum(entry_rows, axis=1) + router_term).astype(jnp.bfloat16)
    grad_router = jnp.dot(dense.T, tokens.astype(jnp.float32), precision=lax.Precision.HIGHEST)
    return (grad_tokens, grad_router, grad_gate, grad_up, grad_down)
```

```python
import functools

import jax
import jax.numpy as jnp
from jax import lax
from jax.experimental import pallas as pl
from jax.experimental.pallas import tpu as pltpu
from jax.sharding import PartitionSpec as P

LANES = 128
SUB = 8
MESH = pl.DeviceIdType.MESH


def remote(src, dst, send, recv, where):
    return pltpu.make_async_remote_copy(
        src_ref=src, dst_ref=dst, send_sem=send, recv_sem=recv, device_id=where, device_id_type=MESH
    )


def greet(n, me, half, both):
    barrier = pltpu.get_barrier_semaphore()

    def step(k, c):
        other = lax.rem(me + k, n)
        pl.semaphore_signal(barrier, inc=1, device_id=(other, half), device_id_type=MESH)
        if both:
            pl.semaphore_signal(barrier, inc=1, device_id=(other, 1 - half), device_id_type=MESH)
        return c

    lax.fori_loop(1, n, step, 0)
    pl.semaphore_signal(barrier, inc=1, device_id=(me, 1 - half), device_id_type=MESH)
    pl.semaphore_wait(barrier, 2 * n - 1 if both else n)


def gather_kernel(n, mine, out, local, send, recv):
    me, half = lax.axis_index("ep"), lax.axis_index("dp")
    own = pltpu.make_async_copy(mine, out.at[me], local)
    own.start()
    greet(n, me, half, False)

    def push(k, c):
        other = lax.rem(me + n - k, n)
        remote(mine, out.at[me], send.at[k], recv.at[k], (other, half)).start()
        return c

    lax.fori_loop(1, n, push, 0)

    def done(k, c):
        source = lax.rem(me + k, n)
        remote(mine, out.at[source], send.at[k], recv.at[k], (source, half)).wait()
        return c

    lax.fori_loop(1, n, done, 0)
    own.wait()


def dispatch_kernel(n, x, g, xa, ga, local, sx, rx, sg, rg, fx, ax, fg, ag):
    me, half = lax.axis_index("ep"), lax.axis_index("dp")
    partner = (me, 1 - half)
    own = pltpu.make_async_copy(x.at[me], xa.at[half, me], local.at[0])
    own_g = pltpu.make_async_copy(g.at[me], ga.at[half, me], local.at[1])
    own.start()
    own_g.start()
    greet(n, me, half, False)

    def push(k, c):
        other = lax.rem(me + n - k, n)
        remote(x.at[other], xa.at[half, me], sx.at[k], rx.at[k], (other, half)).start()
        remote(g.at[other], ga.at[half, me], sg.at[k], rg.at[k], (other, half)).start()
        return c

    lax.fori_loop(1, n, push, 0)
    remote(x.at[me], xa.at[half, me], fx.at[0], ax.at[0], partner).start()
    remote(g.at[me], ga.at[half, me], fg.at[0], ag.at[0], partner).start()

    def relay(k, c):
        source = lax.rem(me + k, n)
        remote(x.at[source], xa.at[half, source], sx.at[k], rx.at[k], partner).wait_recv()
        remote(xa.at[half, source], xa.at[half, source], fx.at[k], ax.at[k], partner).start()
        remote(g.at[source], ga.at[half, source], sg.at[k], rg.at[k], partner).wait_recv()
        remote(ga.at[half, source], ga.at[half, source], fg.at[k], ag.at[k], partner).start()
        return c

    lax.fori_loop(1, n, relay, 0)

    def done(k, c):
        source = lax.rem(me + k, n)
        remote(x.at[me], xa.at[1 - half, source], fx.at[k], ax.at[k], partner).wait()
        remote(g.at[me], ga.at[1 - half, source], fg.at[k], ag.at[k], partner).wait()
        return c

    lax.fori_loop(0, n, done, 0)

    def drain(k, c):
        other = lax.rem(me + n - k, n)
        remote(x.at[other], xa.at[half, me], sx.at[k], rx.at[k], partner).wait_send()
        remote(g.at[other], ga.at[half, me], sg.at[k], rg.at[k], partner).wait_send()
        return c

    lax.fori_loop(1, n, drain, 0)
    own.wait()
    own_g.wait()


def combine_kernel(n, x, g, xb, gb, xin, gin, xs, gs, local, fx, ax, fg, ag, sx, rx, sg, rg):
    me, half = lax.axis_index("ep"), lax.axis_index("dp")
    partner = (me, 1 - half)
    greet(n, me, half, False)

    def give(k, c):
        other = lax.rem(me + n - k, n)
        remote(g.at[1 - half, other], gin.at[other], fg.at[k], ag.at[k], partner).start()
        remote(x.at[1 - half, other], xin.at[other], fx.at[k], ax.at[k], partner).start()
        return c

    lax.fori_loop(0, n, give, 0)

    def add(k, other):
        remote(g.at[1 - half, other], gin.at[other], fg.at[k], ag.at[k], partner).wait()
        gs[other] = g[half, other] + gin[other]
        remote(x.at[1 - half, other], xin.at[other], fx.at[k], ax.at[k], partner).wait()
        xs[other] = (x[half, other].astype(jnp.float32) + xin[other].astype(jnp.float32)).astype(xs.dtype)

    def push(k, c):
        other = lax.rem(me + n - k, n)
        add(k, other)
        remote(gs.at[other], gb.at[me], sg.at[k], rg.at[k], (other, half)).start()
        remote(xs.at[other], xb.at[me], sx.at[k], rx.at[k], (other, half)).start()
        return c

    lax.fori_loop(1, n, push, 0)
    add(0, me)
    own_g = pltpu.make_async_copy(gs.at[me], gb.at[me], local.at[0])
    own = pltpu.make_async_copy(xs.at[me], xb.at[me], local.at[1])
    own_g.start()
    own.start()

    def done(k, c):
        source = lax.rem(me + k, n)
        remote(gs.at[source], gb.at[source], sg.at[k], rg.at[k], (source, half)).wait()
        remote(xs.at[source], xb.at[source], sx.at[k], rx.at[k], (source, half)).wait()
        return c

    lax.fori_loop(1, n, done, 0)
    own_g.wait()
    own.wait()


def router_kernel(n, mine, out, land, near, s0, r0, s1, r1):
    me, half = lax.axis_index("ep"), lax.axis_index("dp")
    greet(n, me, half, True)
    remote(mine.at[me], near.at[me], s1.at[0], r1.at[0], (me, 1 - half)).start()

    def push(k, c):
        other = lax.rem(me + n - k, n)
        remote(mine.at[other], land.at[me], s0.at[k], r0.at[k], (other, half)).start()
        remote(mine.at[other], near.at[me], s1.at[k], r1.at[k], (other, 1 - half)).start()
        return c

    lax.fori_loop(1, n, push, 0)
    remote(mine.at[me], near.at[me], s1.at[0], r1.at[0], (me, 1 - half)).wait()

    def done(k, total):
        source = lax.rem(me + k, n)
        remote(mine.at[source], land.at[source], s0.at[k], r0.at[k], (source, half)).wait()
        remote(mine.at[source], near.at[source], s1.at[k], r1.at[k], (source, 1 - half)).wait()
        return total + (land[source] + near[source])

    out[...] = lax.fori_loop(1, n, done, mine[me] + near[me])


def call(body, n, ident, out_shape, in_spaces, out_spaces, scratch, *args):
    return pl.pallas_call(
        functools.partial(body, n),
        out_shape=out_shape,
        in_specs=[pl.BlockSpec(memory_space=s) for s in in_spaces],
        out_specs=jax.tree.map(lambda s: pl.BlockSpec(memory_space=s), out_spaces),
        scratch_shapes=scratch,
        compiler_params=pltpu.CompilerParams(collective_id=ident, has_side_effects=True),
    )(*args)


def local(tokens, grad_out, assign, router_weight, w_gate, w_up, w_down):
    n = lax.axis_size("ep")
    tok, width = tokens.shape
    experts = n
    need = max(2, (3 * tok + experts - 1) // experts)
    cap = -(-need // SUB) * SUB
    f32, bf = jnp.float32, jnp.bfloat16
    dma = pltpu.SemaphoreType.DMA
    vm, hbm = pltpu.VMEM, pl.ANY
    tile = (SUB, width // SUB)

    router_full = call(
        gather_kernel, n, 0, jax.ShapeDtypeStruct((n,) + tile, f32), [vm], vm,
        [dma(()), dma((n,)), dma((n,))], router_weight.astype(f32).reshape(tile),
    ).reshape(n, width)

    marks = (assign.reshape(-1)[:, None] == jnp.arange(experts, dtype=jnp.int32)[None, :]).astype(f32)
    low = jnp.tril(jnp.ones((2 * tok, 2 * tok), f32), -1)
    before = jnp.dot(low.astype(bf), marks.astype(bf), preferred_element_type=f32)
    ranks = jnp.sum(before * marks, axis=1).astype(jnp.int32)
    slots = (assign.reshape(-1) * cap + ranks).reshape(tok, 2)
    ids = jnp.arange(experts * cap, dtype=jnp.int32)
    hit0 = slots[:, 0][None, :] == ids[:, None]
    hit1 = slots[:, 1][None, :] == ids[:, None]
    pick = (hit0 | hit1).astype(bf)
    stacked = jnp.concatenate([tokens, grad_out], axis=1)
    send = jnp.dot(pick, stacked, preferred_element_type=f32).astype(bf)
    send = send.reshape(experts, cap, 2, width).transpose(0, 2, 1, 3).reshape(experts, 2 * cap, width)

    choose = marks.reshape(tok, 2, experts)
    scores = jnp.dot(tokens, router_full.astype(bf).T, preferred_element_type=f32)
    picked = jnp.sum(scores[:, None, :] * choose, axis=2)
    sig = jax.nn.sigmoid(picked)
    total = jnp.sum(sig, axis=1, keepdims=True)
    gates = sig / total
    low_gates = gates.astype(bf).astype(f32)
    slot_gates = jnp.sum(
        jnp.where(hit0, low_gates[:, 0][None, :], 0.0) + jnp.where(hit1, low_gates[:, 1][None, :], 0.0), axis=1
    ).reshape(experts, 1, cap)
    send_gates = jnp.pad(slot_gates, ((0, 0), (0, SUB - 1), (0, LANES - cap)))

    got, got_gates = call(
        dispatch_kernel, n, 1,
        (jax.ShapeDtypeStruct((2, n, 2 * cap, width), bf), jax.ShapeDtypeStruct((2, n, SUB, LANES), f32)),
        [hbm, hbm], (hbm, hbm),
        [dma((2,))] + [dma((n,))] * 8, send, send_gates,
    )
    rows_total = 2 * n * cap
    rows = got[:, :, :cap].reshape(rows_total, width)
    ups = got[:, :, cap:].reshape(rows_total, width)
    gts = got_gates[:, :, 0, :cap].reshape(rows_total, 1)

    wg, wu, wd = w_gate[0], w_up[0], w_down[0]
    pre_a = jnp.dot(rows, wg, preferred_element_type=f32)
    pre_b = jnp.dot(rows, wu, preferred_element_type=f32)
    sigma = jax.nn.sigmoid(pre_a)
    active = pre_a * sigma
    hid = active * pre_b
    hidden = hid.astype(bf)
    lifted = jnp.dot(ups, wd.T, preferred_element_type=f32)
    part_gates = jnp.sum(hidden.astype(f32) * lifted, axis=1)
    grad_hidden = lifted * gts
    grad_a = (grad_hidden * pre_b * sigma * (1.0 + pre_a * (1.0 - sigma))).astype(bf)
    grad_b = (grad_hidden * active).astype(bf)
    part_rows = jnp.dot(grad_a, wg.T, preferred_element_type=f32) + jnp.dot(
        grad_b, wu.T, preferred_element_type=f32
    )
    scaled = (gts * ups.astype(f32)).astype(bf)

    tiles = jnp.pad(part_gates.reshape(2, n, 1, cap), ((0, 0), (0, 0), (0, SUB - 1), (0, LANES - cap)))
    back_rows, back_gates = call(
        combine_kernel, n, 2,
        (jax.ShapeDtypeStruct((n, cap, width), bf), jax.ShapeDtypeStruct((n, SUB, LANES), f32)),
        [vm, vm], (vm, vm),
        [vm((n, cap, width), bf), vm((n, SUB, LANES), f32), vm((n, cap, width), bf), vm((n, SUB, LANES), f32),
         dma((2,))] + [dma((n,))] * 8,
        part_rows.astype(bf).reshape(2, n, cap, width), tiles,
    )
    turn = (((0,), (0,)), ((), ()))
    grad_gate = lax.dot_general(rows, grad_a, turn, preferred_element_type=f32).astype(bf)[None]
    grad_up = lax.dot_general(rows, grad_b, turn, preferred_element_type=f32).astype(bf)[None]
    grad_down = lax.dot_general(hidden, scaled, turn, preferred_element_type=f32).astype(bf)[None]

    slot_back = back_gates[:, 0, :cap].reshape(1, experts * cap).astype(bf).astype(f32)
    entry0 = jnp.sum(jnp.where(hit0.T, slot_back, 0.0), axis=1)
    entry1 = jnp.sum(jnp.where(hit1.T, slot_back, 0.0), axis=1)
    entry_gates = jnp.stack([entry0, entry1], axis=1)
    mixed = jnp.sum(gates * entry_gates, axis=1, keepdims=True)
    grad_logit = (entry_gates - mixed) / total * sig * (1.0 - sig)
    dense = jnp.sum(grad_logit[:, :, None] * choose, axis=1)
    partial = jnp.dot(dense.T, tokens.astype(f32), precision=lax.Precision.HIGHEST)
    grad_router = call(
        router_kernel, n, 3, jax.ShapeDtypeStruct(tile, f32), [vm], vm,
        [vm((n,) + tile, f32), vm((n,) + tile, f32)] + [dma((n,))] * 4, partial.reshape((n,) + tile),
    ).reshape(1, width)
    entry_sum = jnp.dot(pick.T, back_rows.reshape(experts * cap, width), preferred_element_type=f32)
    router_term = jnp.dot(dense, router_full, precision=lax.Precision.HIGHEST)
    grad_tokens = (entry_sum + router_term).astype(bf)
    return (grad_tokens, grad_router, grad_gate, grad_up, grad_down)


def solution(mesh):
    return jax.shard_map(
        local,
        mesh=mesh,
        in_specs=(
            P(("ep", "dp"), None),
            P(("ep", "dp"), None),
            P(("ep", "dp"), None),
            P("ep", None),
            P("ep", None, "dp"),
            P("ep", None, "dp"),
            P("ep", "dp", None),
        ),
        out_specs=(
            P(("ep", "dp"), None),
            P("ep", None),
            P("ep", None, "dp"),
            P("ep", None, "dp"),
            P("ep", "dp", None),
        ),
        check_vma=False,
    )
```
